32 devices in a mesh: doc: 8 (over z, core), clu: 4 (over y, x).
Axes of the slice: x: 2, y: 2, z: 4, core: 2. Of those that a mesh axis runs over, the one named last changes fastest.
Arguments:
- embeddings: bfloat16 [4096, 256], P(('doc', 'clu')), may hold values from -16 to 16
- centroids: bfloat16 [4096, 256], P('clu'), may hold values from -1 to 1
Outputs:
- new_centroids: float32 [256, 4096], P('doc', 'clu')
- cluster_mass: float32 [4096], P('clu')
The draws below stay inside these ranges and needn't reach their ends.
All inputs are finite; a program needn't handle non-finite values.
Results may differ from the reference program's by a relative error of at most 0.0011.
Values may be sent and summed in bfloat16 or wider, within the bound.
A program may use at most 64 MiB of HBM per device.

```python
import math
import jax
import jax.numpy as jnp
from jax import lax

D = 256
K = 4096
ITERS = 2
DOCS = 4096


def shared_draw(key):
    normal_draw = jax.random.normal(jax.random.fold_in(key, 11), (K, D), jnp.float32)
    centers = jnp.clip(normal_draw, -4.0, 4.0) / jnp.sqrt(jnp.float32(D))
    features_raw = jnp.clip(jax.random.normal(jax.random.fold_in(key, 12), (DOCS, D), jnp.float32), -4.0, 4.0)
    column_scale = 10.0 ** (jnp.arange(D, dtype=jnp.float32) / D) * 0.2157
    embeds = features_raw * column_scale[None, :]
    return (embeds, centers)


def draw_embeddings(key, part):
    return shared_draw(key)[0].astype(jnp.bfloat16)


def draw_centroids(key, part):
    return shared_draw(key)[1].astype(jnp.bfloat16)


def setup_inputs(seed: int = 0) -> dict:
    seeds = jax.random.split(jax.random.key(seed), 3)
    return {
        "embeddings": draw_embeddings(jax.random.fold_in(seeds[2], 71), 0),
        "centroids": draw_centroids(jax.random.fold_in(seeds[2], 71), 0),
    }


entropic_smoothing = 0.05

def reference(embeddings, centroids):
    doc_total = embeddings.shape[0]
    features = embeddings.shape[1]
    cluster_labels = centroids.shape[0]
    block_size = math.gcd(doc_total, 4096)
    block_count = doc_total // block_size
    blocks = embeddings.reshape(block_count, block_size, features)
    log_docs = jnp.log(jnp.float32(doc_total))
    log_clusters = jnp.log(jnp.float32(cluster_labels))

    def scores_of(row_block):
        similarity_energy = lax.dot_general(row_block, centroids, (((1,), (1,)), ((), ())), preferred_element_type=jnp.float32)
        return similarity_energy / entropic_smoothing
    potential = jnp.zeros((block_count, block_size), jnp.float32)
    col_pot = jnp.zeros((cluster_labels,), jnp.float32)
    for iteration in range(ITERS):

        def column_step(state, inputs):
            similarity_energy = scores_of(inputs[0]) + inputs[1][:, None]
            highest = jnp.maximum(state[0], lax.optimization_barrier(jnp.max(similarity_energy, axis=0)))
            expsum = state[1] * jnp.exp(state[0] - highest) + lax.optimization_barrier(jnp.sum(jnp.exp(similarity_energy - highest[None, :]), axis=0))
            return ((highest, expsum), None)
        start_state = (jnp.full((cluster_labels,), -jnp.inf, jnp.float32), jnp.zeros((cluster_labels,), jnp.float32))
        final_state, unused = lax.scan(column_step, start_state, (blocks, potential))
        col_pot = -log_clusters - (final_state[0] + jnp.log(final_state[1]))

        def row_step(row_block):
            similarity_energy = scores_of(row_block) + col_pot[None, :]
            highest = lax.optimization_barrier(jnp.max(similarity_energy, axis=1))
            return -log_docs - (highest + jnp.log(lax.optimization_barrier(jnp.sum(jnp.exp(similarity_energy - highest[:, None]), axis=1))))
        potential = lax.map(row_step, blocks)

    def plan_step(state, inputs):
        plan = jnp.exp(scores_of(inputs[0]) + inputs[1][:, None] + col_pot[None, :] + log_docs)
        mass_part = state[1] + lax.optimization_barrier(jnp.sum(plan, axis=0))
        partial_sum = state[0] + lax.dot_general(inputs[0], plan.astype(jnp.bfloat16), (((0,), (0,)), ((), ())), preferred_element_type=jnp.float32)
        return ((partial_sum, mass_part), None)
    start_state = (jnp.zeros((features, cluster_labels), jnp.float32), jnp.zeros((cluster_labels,), jnp.float32))
    final_state, unused = lax.scan(plan_step, start_state, (blocks, potential))
    summed = final_state[0]
    mean_sq = lax.optimization_barrier(jnp.mean(summed * summed, axis=0))
    new_centroids = summed * lax.rsqrt(mean_sq + 1e-06)
    cluster_mass = final_state[1] * (jnp.float32(cluster_labels) / jnp.float32(doc_total))
    return (new_centroids, cluster_mass)
```

```python
import functools
import math

import jax
import jax.numpy as jnp
from jax import lax
from jax.experimental import pallas as pl
from jax.experimental.pallas import tpu as pltpu
from jax.sharding import PartitionSpec as P

ITERS = 2
SMOOTHING = 0.05
LOG2E = math.log2(math.e)
MESH = pl.DeviceIdType.MESH
F32 = jnp.float32


def kernel(
    nd, nc,
    emb_ref, cent_ref, out_ref, mass_ref,
    emb_all, scores, plan, rpot, colbuf, rowbuf, massbuf, sqbuf, sums, rsbuf, tot, pairbuf,
    own_sem, emb_ss, emb_rs, fwd_ss, col_ss, col_rs, row_ss, row_rs,
    mass_ss, mass_rs, sq_ss, sq_rs, sum_ss, sum_rs, pair_ss, pair_rs,
):
    nz = nd // 2
    nb = 2 * nc
    rows, features = emb_ref.shape
    half = cent_ref.shape[0] // 2
    own_f = features // nd
    log_docs = math.log2(rows * nd * nc)
    log_clusters = math.log2(2 * half * nc)
    d = lax.axis_index("doc")
    c = lax.axis_index("clu")
    core = lax.rem(d, 2)
    z = lax.div(d, 2)
    partner = d + 1 - 2 * core
    me = core * nc + c

    def block_peer(k):
        peer = lax.rem(me + k, nb)
        return peer, (2 * z + lax.div(peer, nc), lax.rem(peer, nc))

    def z_peer(k):
        peer = lax.rem(z + k, nz)
        return peer, (2 * peer + core, c)

    def doc_peer(k):
        peer = lax.rem(d + k, nd)
        return peer, (peer, c)

    def remote(src, dst, ss, rs, device):
        return pltpu.make_async_remote_copy(
            src_ref=src, dst_ref=dst, send_sem=ss, recv_sem=rs,
            device_id=device, device_id_type=MESH,
        )

    sends = []

    def send(*args):
        copy = remote(*args)
        copy.start()
        sends.append(copy)

    barrier = pltpu.get_barrier_semaphore()
    for k in range(1, nb):
        pl.semaphore_signal(barrier, inc=1, device_id=block_peer(k)[1], device_id_type=MESH)
    for k in range(1, nd):
        pl.semaphore_signal(barrier, inc=1, device_id=doc_peer(k)[1], device_id_type=MESH)
    own_copy = pltpu.make_async_copy(emb_ref, emb_all.at[me], own_sem)
    own_copy.start()
    centers = cent_ref[pl.ds(pl.multiple_of(core * half, half), half), :]
    pl.semaphore_wait(barrier, nb - 1 + nd - 1)

    for k in range(1, nc):
        send(emb_ref, emb_all.at[me], emb_ss.at[k], emb_rs.at[me], (d, lax.rem(c + k, nc)))
    send(emb_ref, emb_all.at[me], emb_ss.at[0], emb_rs.at[me], (partner, c))

    def col_update(state, t):
        high, total = state
        t = t.reshape(rows // 8, 8, half)
        new = jnp.maximum(high, jnp.max(t, axis=0))
        total = total * jnp.exp2(high - new) + jnp.sum(jnp.exp2(t - new[None]), axis=0)
        return new, total

    state = (jnp.full((8, half), -jnp.inf, F32), jnp.zeros((8, half), F32))

    def first_block(state, slot):
        s = lax.dot_general(
            emb_all[slot], centers, (((1,), (1,)), ((), ())), preferred_element_type=F32
        ) * (LOG2E / SMOOTHING)
        scores[slot] = s
        return col_update(state, s)

    def arrive(slot):
        remote(
            emb_all.at[slot], emb_all.at[slot], emb_ss.at[0], emb_rs.at[slot], (partner, c)
        ).wait_recv()

    own_copy.wait()
    state = first_block(state, me)
    other = 1 - core
    for k in range(1, nc):
        slot = core * nc + lax.rem(c + k, nc)
        arrive(slot)
        send(emb_all.at[slot], emb_all.at[slot], fwd_ss.at[k], emb_rs.at[slot], (partner, c))
        state = first_block(state, slot)
    for k in range(nc):
        slot = other * nc + lax.rem(c + k, nc)
        arrive(slot)
        state = first_block(state, slot)

    diagonal = lax.broadcasted_iota(jnp.int32, (rows, rows), 0) == lax.broadcasted_iota(
        jnp.int32, (rows, rows), 1
    )

    def to_lanes(x):
        return jnp.sum(jnp.where(diagonal, x, 0.0), axis=0, keepdims=True)

    def to_sublanes(x):
        return jnp.sum(jnp.where(diagonal, x, 0.0), axis=1, keepdims=True)

    def column_potential(it, state):
        high, total = state
        top = jnp.max(high, axis=0, keepdims=True)
        colbuf[it, z, 0:1, :] = top
        colbuf[it, z, 1:2, :] = jnp.sum(total * jnp.exp2(high - top), axis=0, keepdims=True)
        mine = colbuf.at[it, z]
        for k in range(1, nz):
            send(mine, mine, col_ss.at[it, k], col_rs.at[it, z], z_peer(k)[1])
        for k in range(1, nz):
            peer, device = z_peer(k)
            theirs = colbuf.at[it, peer]
            remote(theirs, theirs, col_ss.at[it, k], col_rs.at[it, peer], device).wait_recv()
        tops = [colbuf[it, s, 0:1, :] for s in range(nz)]
        top = functools.reduce(jnp.maximum, tops)
        total = sum(colbuf[it, s, 1:2, :] * jnp.exp2(tops[s] - top) for s in range(nz))
        return -log_clusters - (top + jnp.log2(total))

    def row_potential(it, col_pot):
        def block(b, carry):
            t = scores[b] + col_pot
            high = jnp.max(t, axis=1, keepdims=True)
            total = jnp.sum(jnp.exp2(t - high), axis=1, keepdims=True)
            rowbuf[it, me, pl.ds(b, 1), :] = to_lanes(high)
            rowbuf[it, me, pl.ds(nb + b, 1), :] = to_lanes(total)
            return carry

        lax.fori_loop(0, nb, block, 0)
        mine = rowbuf.at[it, me]
        for k in range(1, nb):
            send(mine, mine, row_ss.at[it, k], row_rs.at[it, me], block_peer(k)[1])
        for k in range(1, nb):
            peer, device = block_peer(k)
            theirs = rowbuf.at[it, peer]
            remote(theirs, theirs, row_ss.at[it, k], row_rs.at[it, peer], device).wait_recv()
        high = rowbuf[it, :, 0:nb, :]
        top = jnp.max(high, axis=0)
        total = jnp.sum(rowbuf[it, :, nb:, :] * jnp.exp2(high - top[None]), axis=0)
        rpot[...] = -log_docs - (top + jnp.log2(total))

    for it in range(ITERS):
        if it > 0:
            def again(b, state):
                return col_update(state, scores[b] + to_sublanes(rpot[pl.ds(b, 1), :]))

            state = lax.fori_loop(
                0, nb, again,
                (jnp.full((8, half), -jnp.inf, F32), jnp.zeros((8, half), F32)),
            )
        col_pot = column_potential(it, state)
        row_potential(it, col_pot)

    def plan_block(b, mass):
        t = scores[b] + to_sublanes(rpot[pl.ds(b, 1), :]) + col_pot + log_docs
        p = jnp.exp2(t)
        plan[pl.ds(pl.multiple_of(b * rows, rows), rows), :] = p.astype(jnp.bfloat16)
        return mass + jnp.sum(p.reshape(rows // 8, 8, half), axis=0)

    mass = lax.fori_loop(0, nb, plan_block, jnp.zeros((8, half), F32))
    sums[...] = lax.dot_general(
        emb_all[...].reshape(nb * rows, features), plan[...],
        (((0,), (0,)), ((), ())), preferred_element_type=F32,
    )
    massbuf[d] = jnp.sum(mass, axis=0, keepdims=True)
    far = sorted(range(1, nz), key=lambda k: -min(k, nz - k))

    def share(peer):
        return sums.at[pl.ds(pl.multiple_of(peer * 2 * own_f, 2 * own_f), 2 * own_f), :]

    for k in far:
        peer, device = z_peer(k)
        send(share(peer), rsbuf.at[z], sum_ss.at[k], sum_rs.at[z], device)
    for k in range(1, nd):
        send(massbuf.at[d], massbuf.at[d], mass_ss.at[k], mass_rs.at[d], doc_peer(k)[1])
    total = share(z)[...]
    for k in reversed(far):
        peer, device = z_peer(k)
        remote(share(z), rsbuf.at[peer], sum_ss.at[k], sum_rs.at[peer], device).wait_recv()
        total = total + rsbuf[peer]
    tot[...] = total
    sqbuf[d] = jnp.sum(total * total, axis=0, keepdims=True)

    def features_of(which):
        return tot.at[pl.ds(pl.multiple_of(which * own_f, own_f), own_f), :]

    for k in range(1, nd):
        send(sqbuf.at[d], sqbuf.at[d], sq_ss.at[k], sq_rs.at[d], doc_peer(k)[1])
    send(features_of(other), pairbuf, pair_ss, pair_rs, (partner, c))
    for k in range(1, nd):
        peer, device = doc_peer(k)
        theirs = massbuf.at[peer]
        remote(theirs, theirs, mass_ss.at[k], mass_rs.at[peer], device).wait_recv()
        theirs = sqbuf.at[peer]
        remote(theirs, theirs, sq_ss.at[k], sq_rs.at[peer], device).wait_recv()
    remote(features_of(core), pairbuf, pair_ss, pair_rs, (partner, c)).wait_recv()

    def finish(which, block):
        columns = pl.ds(pl.multiple_of(which * half, half), half)
        squares = sum(sqbuf[2 * s + which] for s in range(nz))
        out_ref[:, columns] = block * lax.rsqrt(squares / features + 1e-06)
        mass_ref[:, columns] = sum(massbuf[2 * s + which] for s in range(nz)) * (
            2 * half * nc / (rows * nd * nc)
        )

    finish(core, features_of(core)[...])
    finish(other, pairbuf[...])
    for copy in sends:
        copy.wait_send()


def local(nd, nc, embeddings, centroids):
    rows, features = embeddings.shape
    own_cols = centroids.shape[0]
    half, nz, nb = own_cols // 2, nd // 2, 2 * nc
    own_f = features // nd
    dma = pltpu.SemaphoreType.DMA
    out, mass = pl.pallas_call(
        functools.partial(kernel, nd, nc),
        out_shape=(
            jax.ShapeDtypeStruct((own_f, own_cols), F32),
            jax.ShapeDtypeStruct((1, own_cols), F32),
        ),
        in_specs=[pl.BlockSpec(memory_space=pltpu.VMEM)] * 2,
        out_specs=(pl.BlockSpec(memory_space=pltpu.VMEM),) * 2,
        scratch_shapes=[
            pltpu.VMEM((nb, rows, features), jnp.bfloat16),
            pltpu.VMEM((nb, rows, half), F32),
            pltpu.VMEM((nb * rows, half), jnp.bfloat16),
            pltpu.VMEM((nb, rows), F32),
            pltpu.VMEM((ITERS, nz, 2, half), F32),
            pltpu.VMEM((ITERS, nb, 2 * nb, rows), F32),
            pltpu.VMEM((nd, 1, half), F32),
            pltpu.VMEM((nd, 1, half), F32),
            pltpu.VMEM((features, half), F32),
            pltpu.VMEM((nz, 2 * own_f, half), F32),
            pltpu.VMEM((2 * own_f, half), F32),
            pltpu.VMEM((own_f, half), F32),
            dma, dma((nc,)), dma((nb,)), dma((nc,)),
            dma((ITERS, nz)), dma((ITERS, nz)), dma((ITERS, nb)), dma((ITERS, nb)),
            dma((nd,)), dma((nd,)), dma((nd,)), dma((nd,)),
            dma((nz,)), dma((nz,)), dma, dma,
        ],
        compiler_params=pltpu.CompilerParams(
            collective_id=0, has_side_effects=True, vmem_limit_bytes=50 * 2**20
        ),
    )(embeddings, centroids)
    return out, mass.reshape(own_cols)


def solution(mesh):
    placed = (P(("doc", "clu"), None), P("clu", None))
    body = functools.partial(local, mesh.shape["doc"], mesh.shape["clu"])
    return jax.shard_map(
        body, mesh=mesh, in_specs=placed, out_specs=(P("doc", "clu"), P("clu")), check_vma=False
    )
```

```python
import functools
import math

import jax
import jax.numpy as jnp
from jax import lax
from jax.experimental import pallas as pl
from jax.experimental.pallas import tpu as pltpu
from jax.sharding import PartitionSpec as P

ITERS = 2
SMOOTHING = 0.05
LOG2E = math.log2(math.e)
MESH = pl.DeviceIdType.MESH
F32 = jnp.float32


def kernel(
    nd, nc,
    emb_ref, cent_ref, out_ref, mass_ref,
    emb_all, centers, scores, plan, rpot, colbuf, rowbuf, massbuf, sqbuf, sums, rsbuf, tot, pairbuf,
    own_sem, cent_sem, emb_ss, emb_rs, fwd_ss, col_ss, col_rs, row_ss, row_rs,
    mass_ss, mass_rs, sq_ss, sq_rs, sum_ss, sum_rs, pair_ss, pair_rs,
):
    nz = nd // 2
    nb = 2 * nc
    rows, features = emb_ref.shape
    half = cent_ref.shape[0] // 2
    own_f = features // nd
    log_docs = math.log2(rows * nd * nc)
    log_clusters = math.log2(2 * half * nc)
    d = lax.axis_index("doc")
    c = lax.axis_index("clu")
    core = lax.rem(d, 2)
    z = lax.div(d, 2)
    partner = d + 1 - 2 * core
    me = core * nc + c

    def block_peer(k):
        peer = lax.rem(me + k, nb)
        return peer, (2 * z + lax.div(peer, nc), lax.rem(peer, nc))

    def z_peer(k):
        peer = lax.rem(z + k, nz)
        return peer, (2 * peer + core, c)

    def doc_peer(k):
        peer = lax.rem(d + k, nd)
        return peer, (peer, c)

    def remote(src, dst, ss, rs, device):
        return pltpu.make_async_remote_copy(
            src_ref=src, dst_ref=dst, send_sem=ss, recv_sem=rs,
            device_id=device, device_id_type=MESH,
        )

    sends = []

    def send(*args):
        copy = remote(*args)
        copy.start()
        sends.append(copy)

    own_copy = pltpu.make_async_copy(emb_ref, emb_all.at[me], own_sem)
    own_copy.start()
    cent_copy = pltpu.make_async_copy(
        cent_ref.at[pl.ds(pl.multiple_of(core * half, half), half), :], centers, cent_sem
    )
    cent_copy.start()
    barrier = pltpu.get_barrier_semaphore()
    for k in range(1, nb):
        pl.semaphore_signal(barrier, inc=1, device_id=block_peer(k)[1], device_id_type=MESH)
    for k in range(1, nd):
        pl.semaphore_signal(barrier, inc=1, device_id=doc_peer(k)[1], device_id_type=MESH)

    def col_update(state, t):
        high, total = state
        t = t.reshape(rows // 8, 8, half)
        new = jnp.maximum(high, jnp.max(t, axis=0))
        total = total * jnp.exp2(high - new) + jnp.sum(jnp.exp2(t - new[None]), axis=0)
        return new, total

    state = (jnp.full((8, half), -jnp.inf, F32), jnp.zeros((8, half), F32))

    def first_block(state, slot):
        s = lax.dot_general(
            emb_all[slot], centers[...], (((1,), (1,)), ((), ())), preferred_element_type=F32
        ) * (LOG2E / SMOOTHING)
        scores[slot] = s
        return col_update(state, s)

    def arrive(slot):
        remote(
            emb_all.at[slot], emb_all.at[slot], emb_ss.at[0], emb_rs.at[slot], (partner, c)
        ).wait_recv()

    def clu_peer(k):
        if nc & (nc - 1):
            return lax.rem(c + k, nc)
        bits = [1 << i for i in range(nc.bit_length() - 1)]
        return sum(lax.rem(lax.div(c, b) + k // b, 2) * b for b in bits)

    own_copy.wait()
    cent_copy.wait()
    state = first_block(state, me)
    pl.semaphore_wait(barrier, nb - 1 + nd - 1)

    own = emb_all.at[me]
    for k in reversed(range(1, nc)):
        send(own, own, emb_ss.at[k], emb_rs.at[me], (d, clu_peer(k)))
    send(own, own, emb_ss.at[0], emb_rs.at[me], (partner, c))
    other = 1 - core
    for k in range(1, nc):
        slot = core * nc + clu_peer(k)
        arrive(slot)
        send(emb_all.at[slot], emb_all.at[slot], fwd_ss.at[k], emb_rs.at[slot], (partner, c))
        state = first_block(state, slot)
    for k in range(nc):
        slot = other * nc + clu_peer(k)
        arrive(slot)
        state = first_block(state, slot)

    diagonal = lax.broadcasted_iota(jnp.int32, (rows, rows), 0) == lax.broadcasted_iota(
        jnp.int32, (rows, rows), 1
    )

    def to_lanes(x):
        return jnp.sum(jnp.where(diagonal, x, 0.0), axis=0, keepdims=True)

    def to_sublanes(x):
        return jnp.sum(jnp.where(diagonal, x, 0.0), axis=1, keepdims=True)

    def column_potential(it, state):
        high, total = state
        top = jnp.max(high, axis=0, keepdims=True)
        total = jnp.sum(total * jnp.exp2(high - top), axis=0, keepdims=True)
        colbuf[it, z] = top + jnp.log2(total)
        mine = colbuf.at[it, z]
        for k in range(1, nz):
            send(mine, mine, col_ss.at[it, k], col_rs.at[it, z], z_peer(k)[1])
        for k in range(1, nz):
            peer, device = z_peer(k)
            theirs = colbuf.at[it, peer]
            remote(theirs, theirs, col_ss.at[it, k], col_rs.at[it, peer], device).wait_recv()
        logs = [colbuf[it, s] for s in range(nz)]
        top = functools.reduce(jnp.maximum, logs)
        return -log_clusters - (top + jnp.log2(sum(jnp.exp2(x - top) for x in logs)))

    part = nb // 2

    def row_send(it, h, col_pot):
        def block(b, carry):
            t = scores[h * part + b] + col_pot
            high = jnp.max(t, axis=1, keepdims=True)
            total = jnp.sum(jnp.exp2(t - high), axis=1, keepdims=True)
            rowbuf[it, h, me, pl.ds(b, 1), :] = to_lanes(high + jnp.log2(total))
            return carry

        lax.fori_loop(0, part, block, 0, unroll=4)
        mine = rowbuf.at[it, h, me]
        for k in range(1, nb):
            send(mine, mine, row_ss.at[it, h, k], row_rs.at[it, h, me], block_peer(k)[1])

    def row_receive(it, h):
        for k in range(1, nb):
            peer, device = block_peer(k)
            theirs = rowbuf.at[it, h, peer]
            remote(
                theirs, theirs, row_ss.at[it, h, k], row_rs.at[it, h, peer], device
            ).wait_recv()
        logs = rowbuf[it, h]
        top = jnp.max(logs, axis=0)
        total = jnp.sum(jnp.exp2(logs - top[None]), axis=0)
        rpot[h] = -log_docs - (top + jnp.log2(total))

    for it in range(ITERS):
        if it > 0:
            state = (jnp.full((8, half), -jnp.inf, F32), jnp.zeros((8, half), F32))
            for h in range(2):
                def again(b, state):
                    t = scores[h * part + b] + to_sublanes(rpot[h, pl.ds(b, 1), :])
                    return col_update(state, t)

                row_receive(it - 1, h)
                state = lax.fori_loop(0, part, again, state, unroll=4)
        col_pot = column_potential(it, state)
        for h in range(2):
            row_send(it, h, col_pot)

    mass = jnp.zeros((8, half), F32)
    for h in range(2):
        def plan_block(b, mass):
            t = scores[h * part + b] + to_sublanes(rpot[h, pl.ds(b, 1), :]) + col_pot + log_docs
            p = jnp.exp2(t)
            plan[h, pl.ds(pl.multiple_of(b * rows, rows), rows), :] = p.astype(jnp.bfloat16)
            return mass + jnp.sum(p.reshape(rows // 8, 8, half), axis=0)

        row_receive(ITERS - 1, h)
        mass = lax.fori_loop(0, part, plan_block, mass, unroll=4)
        product = lax.dot_general(
            emb_all[h * part:(h + 1) * part].reshape(part * rows, features), plan[h],
            (((0,), (0,)), ((), ())), preferred_element_type=F32,
        )
        sums[...] = product if h == 0 else sums[...] + product
    massbuf[d] = jnp.sum(mass, axis=0, keepdims=True)
    far = sorted(range(1, nz), key=lambda k: -min(k, nz - k))

    def share(peer):
        return sums.at[pl.ds(pl.multiple_of(peer * 2 * own_f, 2 * own_f), 2 * own_f), :]

    for k in far:
        peer, device = z_peer(k)
        send(share(peer), rsbuf.at[z], sum_ss.at[k], sum_rs.at[z], device)
    for k in range(1, nd):
        send(massbuf.at[d], massbuf.at[d], mass_ss.at[k], mass_rs.at[d], doc_peer(k)[1])
    total = share(z)[...]
    for k in reversed(far):
        peer, device = z_peer(k)
        remote(share(z), rsbuf.at[peer], sum_ss.at[k], sum_rs.at[peer], device).wait_recv()
        total = total + rsbuf[peer]
    tot[...] = total
    sqbuf[d] = jnp.sum(total * total, axis=0, keepdims=True)

    def features_of(which):
        return tot.at[pl.ds(pl.multiple_of(which * own_f, own_f), own_f), :]

    for k in range(1, nd):
        send(sqbuf.at[d], sqbuf.at[d], sq_ss.at[k], sq_rs.at[d], doc_peer(k)[1])
    send(features_of(other), pairbuf, pair_ss, pair_rs, (partner, c))
    for k in range(1, nd):
        peer, device = doc_peer(k)
        theirs = massbuf.at[peer]
        remote(theirs, theirs, mass_ss.at[k], mass_rs.at[peer], device).wait_recv()
        theirs = sqbuf.at[peer]
        remote(theirs, theirs, sq_ss.at[k], sq_rs.at[peer], device).wait_recv()
    remote(features_of(core), pairbuf, pair_ss, pair_rs, (partner, c)).wait_recv()

    def finish(which, block):
        columns = pl.ds(pl.multiple_of(which * half, half), half)
        squares = sum(sqbuf[2 * s + which] for s in range(nz))
        out_ref[:, columns] = block * lax.rsqrt(squares / features + 1e-06)
        mass_ref[:, columns] = sum(massbuf[2 * s + which] for s in range(nz)) * (
            2 * half * nc / (rows * nd * nc)
        )

    finish(core, features_of(core)[...])
    finish(other, pairbuf[...])
    for copy in sends:
        copy.wait_send()


def local(nd, nc, embeddings, centroids):
    rows, features = embeddings.shape
    own_cols = centroids.shape[0]
    half, nz, nb = own_cols // 2, nd // 2, 2 * nc
    own_f = features // nd
    dma = pltpu.SemaphoreType.DMA
    out, mass = pl.pallas_call(
        functools.partial(kernel, nd, nc),
        out_shape=(
            jax.ShapeDtypeStruct((own_f, own_cols), F32),
            jax.ShapeDtypeStruct((1, own_cols), F32),
        ),
        in_specs=[pl.BlockSpec(memory_space=pltpu.HBM)] * 2,
        out_specs=(pl.BlockSpec(memory_space=pltpu.VMEM),) * 2,
        scratch_shapes=[
            pltpu.VMEM((nb, rows, features), jnp.bfloat16),
            pltpu.VMEM((half, features), jnp.bfloat16),
            pltpu.VMEM((nb, rows, half), F32),
            pltpu.VMEM((2, nc * rows, half), jnp.bfloat16),
            pltpu.VMEM((2, nc, rows), F32),
            pltpu.VMEM((ITERS, nz, 1, half), F32),
            pltpu.VMEM((ITERS, 2, nb, nc, rows), F32),
            pltpu.VMEM((nd, 1, half), F32),
            pltpu.VMEM((nd, 1, half), F32),
            pltpu.VMEM((features, half), F32),
            pltpu.VMEM((nz, 2 * own_f, half), F32),
            pltpu.VMEM((2 * own_f, half), F32),
            pltpu.VMEM((own_f, half), F32),
            dma, dma, dma((nc,)), dma((nb,)), dma((nc,)),
            dma((ITERS, nz)), dma((ITERS, nz)), dma((ITERS, 2, nb)), dma((ITERS, 2, nb)),
            dma((nd,)), dma((nd,)), dma((nd,)), dma((nd,)),
            dma((nz,)), dma((nz,)), dma, dma,
        ],
        compiler_params=pltpu.CompilerParams(
            collective_id=0, has_side_effects=True
        ),
    )(embeddings, centroids)
    return out, mass.reshape(own_cols)


def solution(mesh):
    placed = (P(("doc", "clu"), None), P("clu", None))
    body = functools.partial(local, mesh.shape["doc"], mesh.shape["clu"])
    return jax.shard_map(
        body, mesh=mesh, in_specs=placed, out_specs=(P("doc", "clu"), P("clu")), check_vma=False
    )
```
